256 devices in a mesh: ctx: 32 (over z, x_hi, core), head: 8 (over y, x_lo).
Axes of the slice: x: 4 (x_hi: 2, x_lo: 2; x = x_hi * 2 + x_lo), y: 4, z: 8, core: 2. Of those that a mesh axis runs over, the one named last changes fastest.
Arguments:
- query_rows: bfloat16 [6144, 8192], P('ctx', 'head'), may hold values from -6 to 6
- key_rows: bfloat16 [6144, 1024], P('ctx', 'head'), may hold values from -6 to 6
- value_rows: bfloat16 [6144, 1024], P('ctx', 'head'), may hold values from -6 to 6
- attn_output: bfloat16 [6144, 8192], P('ctx', 'head'), may hold values from -6 to 6
- log_norms: float32 [64, 6144], P('head', 'ctx'), may hold values from 3 to 5
- grad_output: bfloat16 [6144, 8192], P(('ctx', 'head')), may hold values from -2.390625 to 2.390625
- span_order: int32 [64], replicated, may hold values from 0 to 63, each once
Outputs:
- grad_query: bfloat16 [6144, 8192], P(('ctx', 'head'))
- grad_key: bfloat16 [6144, 1024], P('ctx', 'head')
- grad_value: bfloat16 [6144, 1024], P('ctx', 'head')
The draws below stay inside these ranges and needn't reach their ends.
Inputs may be any that keep to these rules, and one draw needn't show every extreme that they name: span_order is a permutation: each of the 64 spans of 96 positions is held by exactly one slot.
All inputs are finite; a program needn't handle non-finite values.
Results may differ from the reference program's by a relative error of at most 0.0051.
Values may be sent and summed in bfloat16 or wider, within the bound.
No kernel may reach another device: no remote copies, remote signals or barrier semaphores. Data moves between devices by JAX's collectives and lax.ppermute only.
A program may use at most 192 MiB of HBM per device.

```python
import jax
import jax.numpy as jnp
from jax import lax

QH = 64
KVH = 8
HD = 128
TOK_DEV = 192
SPANS = 64
SEQ = 6144


def steps_of(stream_key, shape, cuts, smallest, high):
    gain = 1.0
    for position, blocks in cuts:
        heights = jax.random.uniform(jax.random.fold_in(jax.random.fold_in(stream_key, 6), position), (blocks,), jnp.float32, smallest / len(cuts), high / len(cuts))
        gain = gain * jnp.repeat(jnp.exp(heights), shape[position] // blocks).reshape((-1,) + (1,) * (len(shape) - 1 - position))
    return gain


def centred(own_key, shape, width, bound, pieces=(), kind=jnp.bfloat16):
    result = width * jax.random.normal(own_key, shape, jnp.float32)
    if pieces:
        result = result * steps_of(own_key, shape, pieces, -0.22, 0.18)
    return jnp.clip(result, -bound, bound).astype(kind)


def setup_inputs(seed: int = 0) -> dict:
    splits = jax.random.split(jax.random.key(seed), 8)
    return {
        "query_rows": centred(splits[0], (SEQ, QH * HD), 1.0, 6.0, ((0, 32), (1, 8))),
        "key_rows": centred(splits[1], (SEQ, KVH * HD), 1.0, 6.0, ((0, 32), (1, 8))),
        "value_rows": centred(splits[2], (SEQ, KVH * HD), 1.0, 6.0, ((0, 32), (1, 8))),
        "attn_output": centred(splits[3], (SEQ, QH * HD), 1.0, 6.0, ((0, 32), (1, 8))),
        "log_norms": jnp.clip(3.0 + 2.0 * jax.random.uniform(splits[4], (QH, SEQ), jnp.float32) ** steps_of(splits[4], (QH, SEQ), ((0, 8), (1, 32)), -0.2, 0.2), 3.0, 5.0),
        "grad_output": centred(splits[5], (SEQ, QH * HD), 0.3, 2.390625, ((0, 256),)),
        "span_order": jax.random.permutation(splits[6], SPANS).astype(jnp.int32),
    }


def reference(query_rows, key_rows, value_rows, attn_output, log_norms, grad_output, span_order):
    seq_len = query_rows.shape[0]
    groups = QH // KVH
    half_span = TOK_DEV // 2
    row_ids = jnp.arange(seq_len, dtype=jnp.int32)
    slot_ids = row_ids // half_span
    slot_match = slot_ids[:, None] == jnp.arange(SPANS, dtype=jnp.int32)[None, :]
    span_ids = jnp.sum(jnp.where(slot_match, span_order[None, :], 0), axis=1).astype(jnp.int32)
    positions = span_ids * half_span + row_ids % half_span
    query_heads = query_rows.reshape(seq_len, KVH, groups, HD)
    grad_heads = grad_output.reshape(seq_len, KVH, groups, HD)
    out_heads = attn_output.reshape(seq_len, KVH, groups, HD)
    row_delta = jnp.sum(grad_heads.astype(jnp.float32) * out_heads.astype(jnp.float32), axis=-1)
    lse_rows = log_norms.reshape(KVH, groups, seq_len).transpose(2, 0, 1)
    inv_root = HD ** -0.5
    blocks = seq_len // TOK_DEV

    def one_head(inputs):
        q_head, d_head, delta_head, lse_head, k_head, v_head = inputs
        key_float = k_head.astype(jnp.float32)
        value_float = v_head.astype(jnp.float32)

        def one_block(carry_state, block_id):
            dk_acc, dv_acc = carry_state
            row_start = (block_id * TOK_DEV).astype(jnp.int32)
            q_block = lax.dynamic_slice_in_dim(q_head, row_start, TOK_DEV, 0).astype(jnp.float32)
            d_block = lax.dynamic_slice_in_dim(d_head, row_start, TOK_DEV, 0).astype(jnp.float32)
            delta_block = lax.dynamic_slice_in_dim(delta_head, row_start, TOK_DEV, 0)
            lse_block = lax.dynamic_slice_in_dim(lse_head, row_start, TOK_DEV, 0)
            pos_block = lax.dynamic_slice_in_dim(positions, row_start, TOK_DEV, 0)
            scores = jnp.einsum("tgd,sd->tgs", q_block, key_float) * inv_root
            causal = pos_block[:, None, None] >= positions[None, None, :]
            prob_full = jnp.where(causal, jnp.exp(scores - lse_block[..., None]), 0.0)
            prob_low = lax.optimization_barrier(prob_full.astype(jnp.bfloat16)).astype(jnp.float32)
            dprobs = jnp.einsum("tgd,sd->tgs", d_block, value_float)
            dscores = (prob_full * (dprobs - delta_block[..., None])).astype(jnp.bfloat16)
            dscores = lax.optimization_barrier(dscores).astype(jnp.float32)
            dq_block = jnp.einsum("tgs,sd->tgd", dscores, key_float) * inv_root
            dk_acc = dk_acc + jnp.einsum("tgs,tgd->sd", dscores, q_block) * inv_root
            dv_acc = dv_acc + jnp.einsum("tgs,tgd->sd", prob_low, d_block)
            return (dk_acc, dv_acc), dq_block.astype(jnp.bfloat16)

        empty_acc = jnp.zeros((seq_len, HD), jnp.float32)
        (dk_acc, dv_acc), dq_parts = lax.scan(one_block, (empty_acc, empty_acc), jnp.arange(blocks, dtype=jnp.int32))
        return dq_parts.reshape(seq_len, groups, HD), dk_acc.astype(jnp.bfloat16), dv_acc.astype(jnp.bfloat16)

    dq_all, dk_all, dv_all = lax.map(one_head, (
        query_heads.transpose(1, 0, 2, 3), grad_heads.transpose(1, 0, 2, 3),
        row_delta.transpose(1, 0, 2), lse_rows.transpose(1, 0, 2),
        key_rows.reshape(seq_len, KVH, HD).transpose(1, 0, 2),
        value_rows.reshape(seq_len, KVH, HD).transpose(1, 0, 2)))
    grad_query = dq_all.transpose(1, 0, 2, 3).reshape(seq_len, QH * HD)
    grad_key = dk_all.transpose(1, 0, 2).reshape(seq_len, KVH * HD)
    grad_value = dv_all.transpose(1, 0, 2).reshape(seq_len, KVH * HD)
    return (grad_query, grad_key, grad_value)
```

```python
import functools

import jax
import jax.numpy as jnp
import numpy as np
from jax import lax
from jax.experimental import pallas as pl
from jax.experimental.pallas import tpu as pltpu
from jax.sharding import PartitionSpec as P
HD=128; G=8; SP=96
LOG2E=1.4426950408889634
SC=HD**-0.5
NT=(((1,),(1,)),((),()))
def kernel(nkb, KB, spans, kv_ref, qo_ref, qm_ref, do_ref, dm_ref, lse_ref, del_ref,
           dkv_ref, dq_ref, qs, ds_, kt, dqt, dka, dva):
    for s in range(4):
        src_q, src_d = (qo_ref, do_ref) if s<2 else (qm_ref, dm_ref)
        r0=(s%2)*SP
        for h in range(G):
            qs[pl.ds(s*768+h*SP,SP),:]=src_q[r0:r0+SP, h*HD:(h+1)*HD]
            ds_[pl.ds(s*768+h*SP,SP),:]=src_d[r0:r0+SP, h*HD:(h+1)*HD]
    dqt[...]=jnp.zeros_like(dqt)
    nsp=KB//SP
    def kb_body(kb,_):
        k=kv_ref[kb,:, :HD]
        kt[...]=k.astype(jnp.float32).T.astype(jnp.bfloat16)
        dka[...]=jnp.zeros_like(dka)
        dva[...]=jnp.zeros_like(dva)
        kspan=[spans[4+kb*nsp+j] for j in range(nsp)]
        kmin=functools.reduce(jnp.minimum,kspan)
        kmax=functools.reduce(jnp.maximum,kspan)
        def s_body(s,_):
            rs=spans[s]
            def work(masked):
                row=pl.multiple_of(s*768,768)
                q=qs[pl.ds(row,768),:]
                do=ds_[pl.ds(row,768),:]
                kk=kv_ref[kb,:, :HD]; vv=kv_ref[kb,:, HD:]
                st=lax.dot_general(kk,q,NT,preferred_element_type=jnp.float32)
                p=jnp.exp2(st*(SC*LOG2E)-lse_ref[s])
                if masked:
                    ki=lax.broadcasted_iota(jnp.int32,(KB,1),0)
                    kpos=ki%SP
                    base=jnp.full((KB,1),kspan[0]*SP,jnp.int32)
                    for j in range(1,nsp):
                        base=jnp.where(ki>=j*SP,kspan[j]*SP,base)
                    kpos=kpos+base
                    qpos=lax.broadcasted_iota(jnp.int32,(1,768),1)%SP+rs*SP
                    p=jnp.where(qpos>=kpos,p,0.0)
                dp=lax.dot_general(vv,do,NT,preferred_element_type=jnp.float32)
                dsb=(p*(dp-del_ref[s])).astype(jnp.bfloat16)
                pb=p.astype(jnp.bfloat16)
                dva[...]+=jnp.dot(pb,do,preferred_element_type=jnp.float32)
                dka[...]+=jnp.dot(dsb,q,preferred_element_type=jnp.float32)
                dqt[s]+=jnp.dot(kt[...],dsb,preferred_element_type=jnp.float32)
            @pl.when(kmax<rs)
            def _(): work(False)
            @pl.when((kmax>=rs)&(kmin<=rs))
            def _(): work(True)
            return 0
        lax.fori_loop(0,4,s_body,0)
        dkv_ref[kb,:, :HD]=dka[...]*SC
        dkv_ref[kb,:, HD:]=dva[...]
        return 0
    lax.fori_loop(0,nkb,kb_body,0)
    for s in range(4):
        t=dqt[s].T*SC
        for h in range(G):
            dq_ref[s*SP:(s+1)*SP, h*HD:(h+1)*HD]=t[h*SP:(h+1)*SP,:]

def attn(spans, kv, qo, qm, do, dm, lse, dl, KB):
    nkb=kv.shape[0]
    vm=pl.BlockSpec(memory_space=pltpu.VMEM)
    return pl.pallas_call(
        functools.partial(kernel,nkb,KB),
        out_shape=(jax.ShapeDtypeStruct((nkb,KB,256),jnp.float32), jax.ShapeDtypeStruct((384,1024),jnp.float32)),
        in_specs=[pl.BlockSpec(memory_space=pltpu.SMEM)]+[vm]*7,
        out_specs=(vm,vm),
        scratch_shapes=[pltpu.VMEM((3072,128),jnp.bfloat16)]*2+[pltpu.VMEM((128,KB),jnp.bfloat16),pltpu.VMEM((4,128,768),jnp.float32),
            pltpu.VMEM((KB,128),jnp.float32),pltpu.VMEM((KB,128),jnp.float32)],
        compiler_params=pltpu.CompilerParams(vmem_limit_bytes=56*2**20),
    )(spans,kv,qo,qm,do,dm,lse,dl)


N = 32
CORE = [(i, i ^ 1) for i in range(N)]
XSW = [(i, i ^ 2) for i in range(N)]


def zmap(f):
    return [(i, f(i // 4) * 4 + i % 4) for i in range(N)]


EVEN = zmap(lambda z: z ^ 1)
ODD = zmap(lambda z: (z + 1) % 8 if z % 2 else (z - 1) % 8)


def arrival(first, second):
    f = [dict((s // 4, d // 4) for s, d in m)for m in (first, second)]
    a0 = [[z] for z in range(8)]
    a1 = [a0[f[0][z]] for z in range(8)]
    a2 = [a0[f[1][z]] + a1[f[1][z]] for z in range(8)]
    a3 = [a2[f[0][z]] for z in range(8)]
    a4 = [a3[f[1][z]] for z in range(8)]
    return np.array([a0[z] + a1[z] + a2[z] + a3[z] + a4[z] for z in range(8)], np.int32)


ORDER_A = arrival(EVEN, ODD)
ORDER_B = arrival(ODD, EVEN)


def pp(x, route):
    return lax.ppermute(x, "ctx", route)


def gather(a0, first, second):
    a1 = pp(a0, first)
    a2 = pp(jnp.concatenate([a0, a1]), second)
    a3 = pp(a2, first)
    a4 = pp(a3, second)
    return jnp.concatenate([a0, a1, a2, a3, a4])


def scatter(d, first, second):
    low = lambda x: x.astype(jnp.bfloat16)
    t3 = d[4:6] + pp(low(d[6:8]), second)
    t2 = d[2:4] + pp(low(t3), first)
    t01 = d[0:2] + pp(low(t2), second)
    return t01[0] + pp(low(t01[1]), first)


def per_device(query_rows, key_rows, value_rows, attn_output, log_norms, grad_output, span_order):
    ctx = lax.axis_index("ctx")
    z, x_hi, core = ctx // 4, (ctx // 2) % 2, ctx % 2
    q_mate = pp(query_rows, CORE)
    kv = jnp.concatenate([key_rows, value_rows], axis=1)
    kvx = pp(kv, XSW)
    both = jnp.stack([kv, kvx])
    blocks_a = gather(both[None, :, :SP].reshape(1, 2 * SP, 256), EVEN, ODD)
    blocks_b = gather(both[None, :, SP:].reshape(1, 2 * SP, 256), ODD, EVEN)
    grad_rows = lax.all_to_all(grad_output, "head", split_axis=1, concat_axis=0, tiled=True)
    prod = grad_rows.astype(jnp.float32) * attn_output.astype(jnp.float32)
    delta = jnp.sum(prod.reshape(192, G, HD), axis=-1)
    stats = jnp.stack([
        (log_norms * LOG2E).reshape(G, 2, SP).transpose(1, 0, 2).reshape(2, 1, 768),
        delta.reshape(2, SP, G).transpose(0, 2, 1).reshape(2, 1, 768),
    ], axis=1)
    grad_mate = pp(grad_rows, CORE)
    stats = jnp.concatenate([stats, pp(stats, CORE)])
    kv_all = jnp.concatenate([blocks_a, blocks_b])
    za = jnp.asarray(ORDER_A)[z]
    zb = jnp.asarray(ORDER_B)[z]
    xs = jnp.stack([x_hi, 1 - x_hi])
    slot = lambda zz, j: (((zz[:, None] * 2 + xs[None, :]) * 2 + core) * 2 + j).reshape(-1)
    slots = jnp.concatenate([
        jnp.stack([2 * ctx, 2 * ctx + 1, 2 * (ctx ^ 1), 2 * (ctx ^ 1) + 1]),
        slot(za, 0), slot(zb, 1)])
    spans = span_order[slots]
    dkv, dq = attn(spans, kv_all, query_rows, q_mate, grad_rows, grad_mate, stats[:, 0], stats[:, 1], 192)
    ta = scatter(dkv[:8], EVEN, ODD)
    tb = scatter(dkv[8:], ODD, EVEN)
    t = jnp.stack([ta.reshape(2, SP, 256), tb.reshape(2, SP, 256)], axis=1)
    fin = t[0] + pp(t[1].astype(jnp.bfloat16), XSW)
    fin = fin.reshape(192, 256).astype(jnp.bfloat16)
    dq_own = (dq[:192] + pp(dq[192:].astype(jnp.bfloat16), CORE)).astype(jnp.bfloat16)
    grad_query = lax.all_to_all(dq_own, "head", split_axis=0, concat_axis=1, tiled=True)
    return (grad_query, fin[:, :HD], fin[:, HD:])


def solution(mesh):
    return jax.shard_map(
        per_device,
        mesh=mesh,
        in_specs=(
            P("ctx", "head"),
            P("ctx", "head"),
            P("ctx", "head"),
            P("ctx", "head"),
            P("head", "ctx"),
            P(("ctx", "head"), None),
            P(),
        ),
        out_specs=(P(("ctx", "head"), None), P("ctx", "head"), P("ctx", "head")),
        check_vma=False,
    )
```

```python
import jax
import jax.numpy as jnp
import numpy as np
from jax import lax
from jax.experimental import pallas as pl
from jax.experimental.pallas import tpu as pltpu
from jax.sharding import Mesh
from jax.sharding import PartitionSpec as P

HD = 128
G = 8
SP = 96
ROWS = 192
W = G * SP
KB = 2 * SP
NB = 8
LOG2E = 1.4426950408889634
SC = HD**-0.5
NT = (((1,), (1,)), ((), ()))


def unit(k, v, kt, q, do, lse, delta, kpos, qpos):
    st = lax.dot_general(k, q, NT, preferred_element_type=jnp.float32)
    p = jnp.exp2(st * (SC * LOG2E) - lse)
    if kpos is not None:
        p = jnp.where(qpos >= kpos, p, 0.0)
    dp = lax.dot_general(v, do, NT, preferred_element_type=jnp.float32)
    ds = (p * (dp - delta)).astype(jnp.bfloat16)
    pb = p.astype(jnp.bfloat16)
    dv = jnp.dot(pb, do, preferred_element_type=jnp.float32)
    dk = jnp.dot(ds, q, preferred_element_type=jnp.float32)
    dqt = jnp.dot(kt, ds, preferred_element_type=jnp.float32)
    return dk, dv, dqt


NS = 16
COUNTS = (1, 1, 2, 2, 2)


def kernel(info, a0, a1, a2, a3, a4, q0, q1, q2, q3, d_own, d_mate, lse, delta,
           g0, g1, g2, g3, g4, dq_own, dq_mate, qs, dos, kk, vv, kt, dka, dva, dqt):
    x_hi = info[8]
    for rel, q_src in enumerate((q0, q1, q2, q3)):
        d_src = d_own if rel < 2 else d_mate
        x_abs = x_hi if rel % 2 == 0 else 1 - x_hi
        for s in range(2):
            for h in range(G):
                dst = pl.ds((rel * 2 + s) * W + h * SP, SP)
                qs[dst, :] = q_src[s * SP:(s + 1) * SP, h * HD:(h + 1) * HD]
                dos[dst, :] = d_src[x_abs, s * SP:(s + 1) * SP, h * HD:(h + 1) * HD]

    def spans(refs):
        i = 0
        for ref, n in zip(refs, COUNTS):
            for b in range(n):
                for s in range(2):
                    place = pl.ds(pl.multiple_of(info[9 + NS + i] * SP, SP), SP)
                    yield place, ref, b, slice(s * SP, (s + 1) * SP)
                    i += 1

    for place, ref, b, rows in spans((a0, a1, a2, a3, a4)):
        kk[place, :] = ref[b, rows, :HD]
        vv[place, :] = ref[b, rows, HD:]
    for j in range(NS // 4):
        cols = slice(j * 4 * SP, (j + 1) * 4 * SP)
        kt[:, cols] = kk[cols].astype(jnp.float32).T.astype(jnp.bfloat16)
    dka[...] = jnp.zeros_like(dka)
    dva[...] = jnp.zeros_like(dva)

    def row_span(s, carry):
        span = info[s]
        count = info[9 + 2 * NS + s]
        row = pl.multiple_of(s * W, W)
        dqt[s] = jnp.zeros((HD, W), jnp.float32)

        def work(start, n, masked):
            k0, k1 = start * SP, (start + n) * SP
            kpos = qpos = None
            if masked:
                ki = lax.broadcasted_iota(jnp.int32, (n * SP, 1), 0)
                kpos = ki + info[9 + start] * SP
                for j in range(1, n):
                    kpos = jnp.where(ki >= j * SP, ki + (info[9 + start + j] - j) * SP, kpos)
                qpos = lax.broadcasted_iota(jnp.int32, (1, W), 1) % SP + span * SP
            dk, dv, dq = unit(kk[k0:k1], vv[k0:k1], kt[:, k0:k1], qs[pl.ds(row, W), :], dos[pl.ds(row, W), :],
                              lse[s], delta[s], kpos, qpos)
            dka[k0:k1] += dk
            dva[k0:k1] += dv
            dqt[s] += dq

        for b in range(NS // 4):
            start = 4 * b
            full = info[9 + start + 3] < span

            @pl.when(full)
            def _():
                work(start, 4, False)

            @pl.when((count >= start + 3) & jnp.logical_not(full))
            def _():
                work(start, 4, True)

            @pl.when((count >= start + 1) & (count < start + 3))
            def _():
                work(start, 2, True)

        return carry

    lax.fori_loop(0, 8, row_span, 0)
    for place, ref, b, rows in spans((g0, g1, g2, g3, g4)):
        ref[b, rows, :HD] = (dka[place, :] * SC).astype(ref.dtype)
        ref[b, rows, HD:] = dva[place, :].astype(ref.dtype)
    for rel in range(4):
        x_abs = x_hi if rel % 2 == 0 else 1 - x_hi
        for s in range(2):
            t = dqt[rel * 2 + s].T * SC
            for h in range(G):
                o = t[h * SP:(h + 1) * SP, :]
                if rel < 2:
                    dq_own[x_abs, s * SP:(s + 1) * SP, h * HD:(h + 1) * HD] = o
                else:
                    dq_mate[x_abs, s * SP:(s + 1) * SP, h * HD:(h + 1) * HD] = o.astype(jnp.bfloat16)


def attend(info, keys, qs, d_own, d_mate, lse, delta):
    vm = pl.BlockSpec(memory_space=pltpu.VMEM)
    f32 = jnp.float32
    bf16 = jnp.bfloat16
    out_shape = [jax.ShapeDtypeStruct((n, ROWS, 2 * HD), bf16 if i == 4 else f32) for i, n in enumerate(COUNTS)]
    out_shape += [jax.ShapeDtypeStruct((2, ROWS, G * HD), f32), jax.ShapeDtypeStruct((2, ROWS, G * HD), bf16)]
    scratch = [
        pltpu.VMEM((8 * W, HD), bf16),
        pltpu.VMEM((8 * W, HD), bf16),
        pltpu.VMEM((NS * SP, HD), bf16),
        pltpu.VMEM((NS * SP, HD), bf16),
        pltpu.VMEM((HD, NS * SP), bf16),
        pltpu.VMEM((NS * SP, HD), f32),
        pltpu.VMEM((NS * SP, HD), f32),
        pltpu.VMEM((8, HD, W), f32),
    ]
    return pl.pallas_call(
        kernel,
        out_shape=out_shape,
        in_specs=[pl.BlockSpec(memory_space=pltpu.SMEM)] + [vm] * 13,
        out_specs=[vm] * len(out_shape),
        scratch_shapes=scratch,
        compiler_params=pltpu.CompilerParams(vmem_limit_bytes=48 * 2**20),
        cost_estimate=pl.CostEstimate(flops=16 * 10**9, bytes_accessed=10**7, transcendentals=5 * 10**6),
    )(info, *keys, *qs, d_own, d_mate, lse, delta)


SWAP = [(0, 1), (1, 0)]
EVEN = [(z, z ^ 1) for z in range(8)]
ODD = [(z, (z + 1) % 8 if z % 2 else (z - 1) % 8) for z in range(8)]


def arrival():
    f, g = dict(EVEN), dict(ODD)
    a0 = [[z] for z in range(8)]
    a1 = [a0[f[z]] for z in range(8)]
    a2 = [a0[g[z]] + a1[g[z]] for z in range(8)]
    a3 = [a2[f[z]] for z in range(8)]
    a4 = [a3[g[z]] for z in range(8)]
    return np.array([a0[z] + a1[z] + a2[z] + a3[z] + a4[z] for z in range(8)], np.int32)


ORDER = arrival()


def mate(x):
    return lax.ppermute(x, "core", SWAP)


def across(x):
    return lax.ppermute(x, "x", SWAP)


def along(x, route):
    return lax.ppermute(x, "z", route)


def exchange(x, axes):
    return lax.all_to_all(x, axes, split_axis=0, concat_axis=0, tiled=True)


def table(span_order, row_slots, key_slots, x_hi):
    rows, keys = span_order[row_slots], span_order[key_slots]
    rank = jnp.sum(keys[None, :] < keys[:, None], axis=1)
    hot = rank[None, :] == jnp.arange(NS)[:, None]
    ordered = jnp.sum(jnp.where(hot, keys[None, :], 0), axis=1)
    count = jnp.sum(keys[None, :] <= rows[:, None], axis=1)
    return jnp.concatenate([rows, x_hi[None], ordered, rank, count]).astype(jnp.int32)


def per_device(query_rows, key_rows, value_rows, attn_output, log_norms, grad_output, span_order):
    z, x_hi, core = lax.axis_index("z"), lax.axis_index("x"), lax.axis_index("core")
    f32 = jnp.float32
    bf16 = jnp.bfloat16
    twice = jnp.broadcast_to(grad_output.reshape(1, 24, G, 1024).transpose(0, 2, 1, 3), (2, G, 24, 1024))
    grad_rows = exchange(twice.reshape(16, 24, 1024), ("x", "head")).reshape(2, ROWS, 1024)
    a0 = jnp.concatenate([key_rows, value_rows], axis=1)[None]
    a1 = along(a0, EVEN)
    a2 = along(jnp.concatenate([a0, a1]), ODD)
    a3 = along(a2, EVEN)
    a4 = along(a3, ODD)
    q_x = across(query_rows)
    q_m = mate(query_rows)
    q_mx = mate(q_x)
    mine = lax.dynamic_index_in_dim(grad_rows, x_hi, 0, keepdims=False)
    prod = mine.astype(f32) * attn_output.astype(f32)
    delta = jnp.sum(prod.reshape(ROWS, G, HD), axis=-1)

    def share(t):
        t = jnp.concatenate([t, across(t)])
        return jnp.concatenate([t, mate(t)])

    lse = share((log_norms * LOG2E).reshape(G, 2, SP).transpose(1, 0, 2).reshape(2, 1, W))
    delta = share(delta.reshape(2, SP, G).transpose(0, 2, 1).reshape(2, 1, W))
    grad_mate = mate(grad_rows)
    base = lambda zz, xx, cc: ((zz * 2 + xx) * 2 + cc) * 2
    row_slots = jnp.stack([base(z, xx, cc) + s for cc in (core, 1 - core) for xx in (x_hi, 1 - x_hi) for s in (0, 1)])
    key_slots = base(jnp.asarray(ORDER)[z], x_hi, core)
    key_slots = jnp.stack([key_slots, key_slots + 1], axis=1).reshape(-1)
    info = table(span_order, row_slots, key_slots, x_hi)
    g0, g1, g2, g3, g4, dq_own, dq_mate = attend(
        info, (a0, a1, a2, a3, a4), (query_rows, q_x, q_m, q_mx), grad_rows, grad_mate, lse, delta)
    dq = (dq_own + mate(dq_mate)).astype(bf16).reshape(16, 24, 1024)
    dq = exchange(dq, ("x", "head")).reshape(2, G, 24, 1024)
    t3 = (g3 + along(g4, ODD)).astype(bf16)
    t2 = (g2 + along(t3, EVEN)).astype(bf16)
    r = along(t2, ODD)
    t1 = (g1 + r[1:]).astype(bf16)
    fin = (g0 + r[:1] + along(t1, EVEN)).astype(bf16)[0]
    dq = (dq[0].astype(f32) + dq[1].astype(f32)).astype(bf16)
    grad_query = dq.transpose(1, 0, 2).reshape(24, G * 1024)
    return (grad_query, fin[:, :HD], fin[:, HD:])


def solution(mesh):
    fine = Mesh(mesh.devices.reshape(8, 2, 2, 8), ("z", "x", "core", "head"))
    ctx = ("z", "x", "core")
    return jax.shard_map(
        per_device,
        mesh=fine,
        in_specs=(
            P(ctx, "head"),
            P(ctx, "head"),
            P(ctx, "head"),
            P(ctx, "head"),
            P("head", ctx),
            P(ctx + ("head",), None),
            P(),
        ),
        out_specs=(P(ctx + ("head",), None), P(ctx, "head"), P(ctx, "head")),
        check_vma=False,
    )
```

```python
import jax
import jax.numpy as jnp
import numpy as np
from jax import lax
from jax.experimental import pallas as pl
from jax.experimental.pallas import tpu as pltpu
from jax.sharding import Mesh
from jax.sharding import PartitionSpec as P

HD = 128
G = 8
SP = 96
ROWS = 192
W = G * SP
KB = 2 * SP
NB = 8
LOG2E = 1.4426950408889634
SC = HD**-0.5
NT = (((1,), (1,)), ((), ()))


def unit(k, v, kt, q, do, lse, delta, kpos, qpos):
    st = lax.dot_general(k, q, NT, preferred_element_type=jnp.float32)
    p = jnp.exp2(st * (SC * LOG2E) - lse)
    if kpos is not None:
        p = jnp.where(qpos >= kpos, p, 0.0)
    dp = lax.dot_general(v, do, NT, preferred_element_type=jnp.float32)
    ds = (p * (dp - delta)).astype(jnp.bfloat16)
    pb = p.astype(jnp.bfloat16)
    dv = jnp.dot(pb, do, preferred_element_type=jnp.float32)
    dk = jnp.dot(ds, q, preferred_element_type=jnp.float32)
    dqt = jnp.dot(kt, ds, preferred_element_type=jnp.float32)
    return dk, dv, dqt


NS = 16
COUNTS = (1, 1, 2, 2, 2)


def kernel(info, a0, a1, a2, a3, a4, q0, q1, q2, q3, d_own, d_mate,
           st0, st1, st2, st3, g0, g1, g2, g3, g4, dq_own, dq_mate, qs, dos, kk, vv, kt, dka, dva, dqt, lse, delta):
    x_hi = info[8]
    for rel, st in enumerate((st0, st1, st2, st3)):
        lse[2 * rel:2 * rel + 2] = st[0]
        delta[2 * rel:2 * rel + 2] = st[1]
    for rel, q_src in enumerate((q0, q1, q2, q3)):
        d_src = d_own if rel < 2 else d_mate
        x_abs = x_hi if rel % 2 == 0 else 1 - x_hi
        for s in range(2):
            for h in range(G):
                dst = pl.ds((rel * 2 + s) * W + h * SP, SP)
                qs[dst, :] = q_src[s * SP:(s + 1) * SP, h * HD:(h + 1) * HD]
                dos[dst, :] = d_src[x_abs, s * SP:(s + 1) * SP, h * HD:(h + 1) * HD]

    def spans(refs):
        i = 0
        for ref, n in zip(refs, COUNTS):
            for b in range(n):
                for s in range(2):
                    place = pl.ds(pl.multiple_of(info[9 + NS + i] * SP, SP), SP)
                    yield place, ref, b, slice(s * SP, (s + 1) * SP)
                    i += 1

    for place, ref, b, rows in spans((a0, a1, a2, a3, a4)):
        kk[place, :] = ref[b, rows, :HD]
        vv[place, :] = ref[b, rows, HD:]
    for j in range(NS // 4):
        cols = slice(j * 4 * SP, (j + 1) * 4 * SP)
        kt[:, cols] = kk[cols].astype(jnp.float32).T.astype(jnp.bfloat16)
    dka[...] = jnp.zeros_like(dka)
    dva[...] = jnp.zeros_like(dva)

    def row_span(s, carry):
        span = info[s]
        count = info[9 + 2 * NS + s]
        row = pl.multiple_of(s * W, W)
        dqt[s] = jnp.zeros((HD, W), jnp.float32)

        def work(start, n, masked):
            k0, k1 = start * SP, (start + n) * SP
            kpos = qpos = None
            if masked:
                ki = lax.broadcasted_iota(jnp.int32, (n * SP, 1), 0)
                kpos = ki + info[9 + start] * SP
                for j in range(1, n):
                    kpos = jnp.where(ki >= j * SP, ki + (info[9 + start + j] - j) * SP, kpos)
                qpos = lax.broadcasted_iota(jnp.int32, (1, W), 1) % SP + span * SP
            dk, dv, dq = unit(kk[k0:k1], vv[k0:k1], kt[:, k0:k1], qs[pl.ds(row, W), :], dos[pl.ds(row, W), :],
                              lse[s], delta[s], kpos, qpos)
            dka[k0:k1] += dk
            dva[k0:k1] += dv
            dqt[s] += dq

        for b in range(NS // 4):
            start = 4 * b
            full = info[9 + start + 3] < span

            @pl.when(full)
            def _():
                work(start, 4, False)

            @pl.when((count >= start + 3) & jnp.logical_not(full))
            def _():
                work(start, 4, True)

            @pl.when((count >= start + 1) & (count < start + 3))
            def _():
                work(start, 2, True)

        return carry

    lax.fori_loop(0, 8, row_span, 0)
    for place, ref, b, rows in spans((g0, g1, g2, g3, g4)):
        ref[b, rows, :HD] = (dka[place, :] * SC).astype(ref.dtype)
        ref[b, rows, HD:] = dva[place, :].astype(ref.dtype)
    for rel in range(4):
        x_abs = x_hi if rel % 2 == 0 else 1 - x_hi
        for s in range(2):
            t = dqt[rel * 2 + s].T * SC
            for h in range(G):
                o = t[h * SP:(h + 1) * SP, :]
                if rel < 2:
                    dq_own[x_abs, s * SP:(s + 1) * SP, h * HD:(h + 1) * HD] = o
                else:
                    dq_mate[x_abs, s * SP:(s + 1) * SP, h * HD:(h + 1) * HD] = o.astype(jnp.bfloat16)


def attend(info, keys, qs, d_own, d_mate, stats):
    vm = pl.BlockSpec(memory_space=pltpu.VMEM)
    f32 = jnp.float32
    bf16 = jnp.bfloat16
    out_shape = [jax.ShapeDtypeStruct((n, ROWS, 2 * HD), bf16 if i == 4 else f32) for i, n in enumerate(COUNTS)]
    out_shape += [jax.ShapeDtypeStruct((2, ROWS, G * HD), f32), jax.ShapeDtypeStruct((2, ROWS, G * HD), bf16)]
    scratch = [
        pltpu.VMEM((8 * W, HD), bf16),
        pltpu.VMEM((8 * W, HD), bf16),
        pltpu.VMEM((NS * SP, HD), bf16),
        pltpu.VMEM((NS * SP, HD), bf16),
        pltpu.VMEM((HD, NS * SP), bf16),
        pltpu.VMEM((NS * SP, HD), f32),
        pltpu.VMEM((NS * SP, HD), f32),
        pltpu.VMEM((8, HD, W), f32),
        pltpu.VMEM((8, 1, W), f32),
        pltpu.VMEM((8, 1, W), f32),
    ]
    return pl.pallas_call(
        kernel,
        out_shape=out_shape,
        in_specs=[pl.BlockSpec(memory_space=pltpu.SMEM)] + [vm] * 15,
        out_specs=[vm] * len(out_shape),
        scratch_shapes=scratch,
        compiler_params=pltpu.CompilerParams(vmem_limit_bytes=24 * 2**20),
        cost_estimate=pl.CostEstimate(flops=16 * 10**9, bytes_accessed=10**7, transcendentals=5 * 10**6),
    )(info, *keys, *qs, d_own, d_mate, *stats)


def prepare(grad, keys, values, out, a0):
    for x in range(2):
        for h in range(G):
            out[x * G + h] = grad[:, h * 1024:(h + 1) * 1024]
    a0[0, :, :HD] = keys[...]
    a0[0, :, HD:] = values[...]


def row_stats(x_hi, grad, attn, lse, out, prod):
    bf16 = jnp.bfloat16
    for s in range(2):
        rows = slice(s * SP, (s + 1) * SP)
        for h in range(G):
            cols = slice(h * HD, (h + 1) * HD)
            prod[h * SP:(h + 1) * SP] = grad[x_hi[0], rows, cols].astype(jnp.float32) * attn[rows, cols].astype(jnp.float32)
        full = prod[...]
        high = full.astype(bf16)
        low = (full - high.astype(jnp.float32)).astype(bf16)
        ones = jnp.ones((8, HD), bf16)
        sums = lax.dot_general(ones, high, NT, preferred_element_type=jnp.float32)
        sums += lax.dot_general(ones, low, NT, preferred_element_type=jnp.float32)
        out[1, s] = sums[:1]
        out[0, s] = lse[s]


SWAP = [(0, 1), (1, 0)]
EVEN = [(z, z ^ 1) for z in range(8)]
ODD = [(z, (z + 1) % 8 if z % 2 else (z - 1) % 8) for z in range(8)]


def arrival():
    f, g = dict(EVEN), dict(ODD)
    a0 = [[z] for z in range(8)]
    a1 = [a0[f[z]] for z in range(8)]
    a2 = [a0[g[z]] + a1[g[z]] for z in range(8)]
    a3 = [a2[f[z]] for z in range(8)]
    a4 = [a3[g[z]] for z in range(8)]
    return np.array([a0[z] + a1[z] + a2[z] + a3[z] + a4[z] for z in range(8)], np.int32)


ORDER = arrival()


def mate(x):
    return lax.ppermute(x, "core", SWAP)


def across(x):
    return lax.ppermute(x, "x", SWAP)


def along(x, route):
    return lax.ppermute(x, "z", route)


def exchange(x, axes):
    return lax.all_to_all(x, axes, split_axis=0, concat_axis=0, tiled=True)


def table(span_order, row_slots, key_slots, x_hi):
    rows, keys = span_order[row_slots], span_order[key_slots]
    rank = jnp.sum(keys[None, :] < keys[:, None], axis=1)
    hot = rank[None, :] == jnp.arange(NS)[:, None]
    ordered = jnp.sum(jnp.where(hot, keys[None, :], 0), axis=1)
    count = jnp.sum(keys[None, :] <= rows[:, None], axis=1)
    return jnp.concatenate([rows, x_hi[None], ordered, rank, count]).astype(jnp.int32)


def per_device(query_rows, key_rows, value_rows, attn_output, log_norms, grad_output, span_order):
    z, x_hi, core = lax.axis_index("z"), lax.axis_index("x"), lax.axis_index("core")
    f32 = jnp.float32
    bf16 = jnp.bfloat16
    base = lambda zz, xx, cc: ((zz * 2 + xx) * 2 + cc) * 2
    row_slots = jnp.stack([base(z, xx, cc) + s for cc in (core, 1 - core) for xx in (x_hi, 1 - x_hi) for s in (0, 1)])
    key_slots = base(jnp.asarray(ORDER)[z], x_hi, core)
    key_slots = jnp.stack([key_slots, key_slots + 1], axis=1).reshape(-1)
    info = table(span_order, row_slots, key_slots, x_hi)
    vm = pl.BlockSpec(memory_space=pltpu.VMEM)
    twice, a0 = pl.pallas_call(
        prepare,
        out_shape=(jax.ShapeDtypeStruct((16, 24, 1024), bf16), jax.ShapeDtypeStruct((1, ROWS, 2 * HD), bf16)),
        in_specs=[vm] * 3,
        out_specs=(vm, vm),
    )(grad_output, key_rows, value_rows)
    grad_rows = exchange(twice, ("x", "head")).reshape(2, ROWS, 1024)
    a1 = along(a0, EVEN)
    a2 = along(jnp.concatenate([a0, a1]), ODD)
    lse = (log_norms * LOG2E).reshape(G, 2, SP).transpose(1, 0, 2).reshape(2, 1, W)
    grad_rows, a2, info, lse = lax.optimization_barrier((grad_rows, a2, info, lse))
    a3 = along(a2, EVEN)
    q_x = across(query_rows)
    q_m = mate(query_rows)
    q_mx = mate(q_x)
    stats = pl.pallas_call(
        row_stats,
        out_shape=jax.ShapeDtypeStruct((2, 2, 1, W), f32),
        in_specs=[pl.BlockSpec(memory_space=pltpu.SMEM), vm, vm, vm],
        out_specs=vm,
        scratch_shapes=[pltpu.VMEM((W, HD), f32)],
    )(x_hi[None].astype(jnp.int32), grad_rows, attn_output, lse)
    stats, a3 = lax.optimization_barrier((stats, a3))
    a4 = along(a3, ODD)
    grad_mate = mate(grad_rows)
    stats_x = across(stats)
    stats_x, a4 = lax.optimization_barrier((stats_x, a4))
    stats = (stats, stats_x, mate(stats), mate(stats_x))
    g0, g1, g2, g3, g4, dq_own, dq_mate = attend(
        info, (a0, a1, a2, a3, a4), (query_rows, q_x, q_m, q_mx), grad_rows, grad_mate, stats)
    r = along(g4, ODD)
    dq = (dq_own + mate(dq_mate)).astype(bf16).reshape(16, 24, 1024)
    r, dq = lax.optimization_barrier((r, dq))
    dq = exchange(dq, ("x", "head")).reshape(2, G, 24, 1024)
    t3 = (g3 + r).astype(bf16)
    t2 = (g2 + along(t3, EVEN)).astype(bf16)
    r = along(t2, ODD)
    t1 = (g1 + r[1:]).astype(bf16)
    t1, dq = lax.optimization_barrier((t1, dq))
    fin = (g0 + r[:1] + along(t1, EVEN)).astype(bf16)[0]
    dq = (dq[0].astype(f32) + dq[1].astype(f32)).astype(bf16)
    grad_query = dq.transpose(1, 0, 2).reshape(24, G * 1024)
    return (grad_query, fin[:, :HD], fin[:, HD:])


def solution(mesh):
    fine = Mesh(mesh.devices.reshape(8, 2, 2, 8), ("z", "x", "core", "head"))
    ctx = ("z", "x", "core")
    return jax.shard_map(
        per_device,
        mesh=fine,
        in_specs=(
            P(ctx, "head"),
            P(ctx, "head"),
            P(ctx, "head"),
            P(ctx, "head"),
            P("head", ctx),
            P(ctx + ("head",), None),
            P(),
        ),
        out_specs=(P(ctx + ("head",), None), P(ctx, "head"), P(ctx, "head")),
        check_vma=False,
    )
```

```python
import jax
import jax.numpy as jnp
import numpy as np
from jax import lax
from jax.experimental import pallas as pl
from jax.experimental.pallas import tpu as pltpu
from jax.sharding import Mesh
from jax.sharding import PartitionSpec as P

HD = 128
G = 8
SP = 96
ROWS = 192
W = G * SP
KB = 2 * SP
NB = 8
LOG2E = 1.4426950408889634
SC = HD**-0.5
NT = (((1,), (1,)), ((), ()))


def unit(k, v, kt, q, do, lse, delta, kpos, qpos):
    st = lax.dot_general(k, q, NT, preferred_element_type=jnp.float32)
    p = jnp.exp2(st * (SC * LOG2E) - lse)
    if kpos is not None:
        p = jnp.where(qpos >= kpos, p, 0.0)
    dp = lax.dot_general(v, do, NT, preferred_element_type=jnp.float32)
    ds = (p * (dp - delta)).astype(jnp.bfloat16)
    pb = p.astype(jnp.bfloat16)
    dv = jnp.dot(pb, do, preferred_element_type=jnp.float32)
    dk = jnp.dot(ds, q, preferred_element_type=jnp.float32)
    dqt = jnp.dot(kt, ds, preferred_element_type=jnp.float32)
    return dk, dv, dqt


NS = 16
COUNTS = (1, 1, 2, 2, 2)


def kernel(info, a0, a1, a2, a3, a4, q0, q1, q2, q3, d_own, d_mate,
           st0, st1, st2, st3, g0, g1, g2, g3, g4, dq_own, dq_mate, qs, dos, kk, vv, kt, dka, dva, dqt, lse, delta):
    x_hi = info[8]
    for rel, st in enumerate((st0, st1, st2, st3)):
        lse[2 * rel:2 * rel + 2] = st[0]
        delta[2 * rel:2 * rel + 2] = st[1]
    for rel, q_src in enumerate((q0, q1, q2, q3)):
        d_src = d_own if rel < 2 else d_mate
        x_abs = x_hi if rel % 2 == 0 else 1 - x_hi
        for s in range(2):
            for h in range(G):
                dst = pl.ds((rel * 2 + s) * W + h * SP, SP)
                qs[dst, :] = q_src[s * SP:(s + 1) * SP, h * HD:(h + 1) * HD]
                dos[dst, :] = d_src[x_abs, s * SP:(s + 1) * SP, h * HD:(h + 1) * HD]

    def spans(refs):
        i = 0
        for ref, n in zip(refs, COUNTS):
            for b in range(n):
                for s in range(2):
                    place = pl.ds(pl.multiple_of(info[9 + NS + i] * SP, SP), SP)
                    yield place, ref, b, slice(s * SP, (s + 1) * SP)
                    i += 1

    for place, ref, b, rows in spans((a0, a1, a2, a3, a4)):
        kk[place, :] = ref[b, rows, :HD]
        vv[place, :] = ref[b, rows, HD:]
    for j in range(NS // 4):
        cols = slice(j * 4 * SP, (j + 1) * 4 * SP)
        kt[:, cols] = kk[cols].astype(jnp.float32).T.astype(jnp.bfloat16)
    dka[...] = jnp.zeros_like(dka)
    dva[...] = jnp.zeros_like(dva)

    def row_span(s, carry):
        span = info[s]
        count = info[9 + 2 * NS + s]
        row = pl.multiple_of(s * W, W)
        dqt[s] = jnp.zeros((HD, W), jnp.float32)

        def work(start, n, masked):
            k0, k1 = start * SP, (start + n) * SP
            kpos = qpos = None
            if masked:
                ki = lax.broadcasted_iota(jnp.int32, (n * SP, 1), 0)
                kpos = ki + info[9 + start] * SP
                for j in range(1, n):
                    kpos = jnp.where(ki >= j * SP, ki + (info[9 + start + j] - j) * SP, kpos)
                qpos = lax.broadcasted_iota(jnp.int32, (1, W), 1) % SP + span * SP
            dk, dv, dq = unit(kk[k0:k1], vv[k0:k1], kt[:, k0:k1], qs[pl.ds(row, W), :], dos[pl.ds(row, W), :],
                              lse[s], delta[s], kpos, qpos)
            dka[k0:k1] += dk
            dva[k0:k1] += dv
            dqt[s] += dq

        for c in range(NS // 8):
            whole = info[9 + 8 * c + 7] < span

            @pl.when(whole)
            def _():
                work(8 * c, 8, False)

            @pl.when(jnp.logical_not(whole))
            def _():
                for start in (8 * c, 8 * c + 4):
                    full = info[9 + start + 3] < span

                    @pl.when(full)
                    def _():
                        work(start, 4, False)

                    @pl.when((count >= start + 3) & jnp.logical_not(full))
                    def _():
                        work(start, 4, True)

                    @pl.when((count >= start + 1) & (count < start + 3))
                    def _():
                        work(start, 2, True)

        return carry

    lax.fori_loop(0, 8, row_span, 0)
    for place, ref, b, rows in spans((g0, g1, g2, g3, g4)):
        ref[b, rows, :HD] = (dka[place, :] * SC).astype(ref.dtype)
        ref[b, rows, HD:] = dva[place, :].astype(ref.dtype)
    for rel in range(4):
        x_abs = x_hi if rel % 2 == 0 else 1 - x_hi
        for s in range(2):
            t = dqt[rel * 2 + s].T * SC
            for h in range(G):
                o = t[h * SP:(h + 1) * SP, :]
                if rel < 2:
                    dq_own[x_abs, s * SP:(s + 1) * SP, h * HD:(h + 1) * HD] = o
                else:
                    dq_mate[x_abs, s * SP:(s + 1) * SP, h * HD:(h + 1) * HD] = o.astype(jnp.bfloat16)


def attend(info, keys, qs, d_own, d_mate, stats):
    vm = pl.BlockSpec(memory_space=pltpu.VMEM)
    f32 = jnp.float32
    bf16 = jnp.bfloat16
    out_shape = [jax.ShapeDtypeStruct((n, ROWS, 2 * HD), bf16 if i == 4 else f32) for i, n in enumerate(COUNTS)]
    out_shape += [jax.ShapeDtypeStruct((2, ROWS, G * HD), f32), jax.ShapeDtypeStruct((2, ROWS, G * HD), bf16)]
    scratch = [
        pltpu.VMEM((8 * W, HD), bf16),
        pltpu.VMEM((8 * W, HD), bf16),
        pltpu.VMEM((NS * SP, HD), bf16),
        pltpu.VMEM((NS * SP, HD), bf16),
        pltpu.VMEM((HD, NS * SP), bf16),
        pltpu.VMEM((NS * SP, HD), f32),
        pltpu.VMEM((NS * SP, HD), f32),
        pltpu.VMEM((8, HD, W), f32),
        pltpu.VMEM((8, 1, W), f32),
        pltpu.VMEM((8, 1, W), f32),
    ]
    return pl.pallas_call(
        kernel,
        out_shape=out_shape,
        in_specs=[pl.BlockSpec(memory_space=pltpu.SMEM)] + [vm] * 15,
        out_specs=[vm] * len(out_shape),
        scratch_shapes=scratch,
        compiler_params=pltpu.CompilerParams(vmem_limit_bytes=32 * 2**20),
        cost_estimate=pl.CostEstimate(flops=16 * 10**9, bytes_accessed=10**7, transcendentals=5 * 10**6),
    )(info, *keys, *qs, d_own, d_mate, *stats)


def prepare(grad, keys, values, out, a0):
    for x in range(2):
        for h in range(G):
            out[x * G + h] = grad[:, h * 1024:(h + 1) * 1024]
    a0[0, :, :HD] = keys[...]
    a0[0, :, HD:] = values[...]


def row_stats(x_hi, grad, attn, lse, out, prod):
    bf16 = jnp.bfloat16
    for s in range(2):
        rows = slice(s * SP, (s + 1) * SP)
        for h in range(G):
            cols = slice(h * HD, (h + 1) * HD)
            prod[h * SP:(h + 1) * SP] = grad[x_hi[0], rows, cols].astype(jnp.float32) * attn[rows, cols].astype(jnp.float32)
        full = prod[...]
        high = full.astype(bf16)
        low = (full - high.astype(jnp.float32)).astype(bf16)
        ones = jnp.ones((8, HD), bf16)
        sums = lax.dot_general(ones, high, NT, preferred_element_type=jnp.float32)
        sums += lax.dot_general(ones, low, NT, preferred_element_type=jnp.float32)
        out[1, s] = sums[:1]
        out[0, s] = lse[s]


SWAP = [(0, 1), (1, 0)]
EVEN = [(z, z ^ 1) for z in range(8)]
ODD = [(z, (z + 1) % 8 if z % 2 else (z - 1) % 8) for z in range(8)]


def arrival():
    f, g = dict(EVEN), dict(ODD)
    a0 = [[z] for z in range(8)]
    a1 = [a0[f[z]] for z in range(8)]
    a2 = [a0[g[z]] + a1[g[z]] for z in range(8)]
    a3 = [a2[f[z]] for z in range(8)]
    a4 = [a3[g[z]] for z in range(8)]
    return np.array([a0[z] + a1[z] + a2[z] + a3[z] + a4[z] for z in range(8)], np.int32)


ORDER = arrival()


def mate(x):
    return lax.ppermute(x, "core", SWAP)


def across(x):
    return lax.ppermute(x, "x", SWAP)


def along(x, route):
    return lax.ppermute(x, "z", route)


def exchange(x, axes):
    return lax.all_to_all(x, axes, split_axis=0, concat_axis=0, tiled=True)


def table(span_order, row_slots, key_slots, x_hi):
    rows, keys = span_order[row_slots], span_order[key_slots]
    rank = jnp.sum(keys[None, :] < keys[:, None], axis=1)
    hot = rank[None, :] == jnp.arange(NS)[:, None]
    ordered = jnp.sum(jnp.where(hot, keys[None, :], 0), axis=1)
    count = jnp.sum(keys[None, :] <= rows[:, None], axis=1)
    return jnp.concatenate([rows, x_hi[None], ordered, rank, count]).astype(jnp.int32)


def per_device(query_rows, key_rows, value_rows, attn_output, log_norms, grad_output, span_order):
    z, x_hi, core = lax.axis_index("z"), lax.axis_index("x"), lax.axis_index("core")
    f32 = jnp.float32
    bf16 = jnp.bfloat16
    base = lambda zz, xx, cc: ((zz * 2 + xx) * 2 + cc) * 2
    row_slots = jnp.stack([base(z, xx, cc) + s for cc in (core, 1 - core) for xx in (x_hi, 1 - x_hi) for s in (0, 1)])
    key_slots = base(jnp.asarray(ORDER)[z], x_hi, core)
    key_slots = jnp.stack([key_slots, key_slots + 1], axis=1).reshape(-1)
    info = table(span_order, row_slots, key_slots, x_hi)
    vm = pl.BlockSpec(memory_space=pltpu.VMEM)
    twice, a0 = pl.pallas_call(
        prepare,
        out_shape=(jax.ShapeDtypeStruct((16, 24, 1024), bf16), jax.ShapeDtypeStruct((1, ROWS, 2 * HD), bf16)),
        in_specs=[vm] * 3,
        out_specs=(vm, vm),
    )(grad_output, key_rows, value_rows)
    grad_rows = exchange(twice, ("x", "head")).reshape(2, ROWS, 1024)
    a1 = along(a0, EVEN)
    a2 = along(jnp.concatenate([a0, a1]), ODD)
    lse = (log_norms * LOG2E).reshape(G, 2, SP).transpose(1, 0, 2).reshape(2, 1, W)
    grad_rows, a2, info, lse = lax.optimization_barrier((grad_rows, a2, info, lse))
    a3 = along(a2, EVEN)
    q_x = across(query_rows)
    q_m = mate(query_rows)
    q_mx = mate(q_x)
    stats = pl.pallas_call(
        row_stats,
        out_shape=jax.ShapeDtypeStruct((2, 2, 1, W), f32),
        in_specs=[pl.BlockSpec(memory_space=pltpu.SMEM), vm, vm, vm],
        out_specs=vm,
        scratch_shapes=[pltpu.VMEM((W, HD), f32)],
        compiler_params=pltpu.CompilerParams(vmem_limit_bytes=8 * 2**20),
    )(x_hi[None].astype(jnp.int32), grad_rows, attn_output, lse)
    stats_x = across(stats)
    stats_x, a3 = lax.optimization_barrier((stats_x, a3))
    a4 = along(a3, ODD)
    grad_mate = mate(grad_rows)
    stats = (stats, stats_x, mate(stats), mate(stats_x))
    g0, g1, g2, g3, g4, dq_own, dq_mate = attend(
        info, (a0, a1, a2, a3, a4), (query_rows, q_x, q_m, q_mx), grad_rows, grad_mate, stats)
    r = along(g4, ODD)
    dq = (dq_own + mate(dq_mate)).astype(bf16).reshape(16, 24, 1024)
    r, dq = lax.optimization_barrier((r, dq))
    dq = exchange(dq, ("x", "head")).reshape(2, G, 24, 1024)
    t3 = (g3 + r).astype(bf16)
    t2 = (g2 + along(t3, EVEN)).astype(bf16)
    r = along(t2, ODD)
    t1 = (g1 + r[1:]).astype(bf16)
    t1, dq = lax.optimization_barrier((t1, dq))
    fin = (g0 + r[:1] + along(t1, EVEN)).astype(bf16)[0]
    dq = (dq[0].astype(f32) + dq[1].astype(f32)).astype(bf16)
    grad_query = dq.transpose(1, 0, 2).reshape(24, G * 1024)
    return (grad_query, fin[:, :HD], fin[:, HD:])


def solution(mesh):
    fine = Mesh(mesh.devices.reshape(8, 2, 2, 8), ("z", "x", "core", "head"))
    ctx = ("z", "x", "core")
    return jax.shard_map(
        per_device,
        mesh=fine,
        in_specs=(
            P(ctx, "head"),
            P(ctx, "head"),
            P(ctx, "head"),
            P(ctx, "head"),
            P("head", ctx),
            P(ctx + ("head",), None),
            P(),
        ),
        out_specs=(P(ctx + ("head",), None), P(ctx, "head"), P(ctx, "head")),
        check_vma=False,
    )
```

```python
import jax
import jax.numpy as jnp
import numpy as np
from jax import lax
from jax.experimental import pallas as pl
from jax.experimental.pallas import tpu as pltpu
from jax.sharding import Mesh
from jax.sharding import PartitionSpec as P

HD = 128
G = 8
SP = 96
ROWS = 192
W = G * SP
KB = 2 * SP
NB = 8
LOG2E = 1.4426950408889634
SC = HD**-0.5
NT = (((1,), (1,)), ((), ()))


def unit(k, v, kt, q, do, lse, delta, kpos, qpos):
    st = lax.dot_general(k, q, NT, preferred_element_type=jnp.float32)
    p = jnp.exp2(st * (SC * LOG2E) - lse)
    if kpos is not None:
        p = jnp.where(qpos >= kpos, p, 0.0)
    dp = lax.dot_general(v, do, NT, preferred_element_type=jnp.float32)
    ds = (p * (dp - delta)).astype(jnp.bfloat16)
    pb = p.astype(jnp.bfloat16)
    dv = jnp.dot(pb, do, preferred_element_type=jnp.float32)
    dk = jnp.dot(ds, q, preferred_element_type=jnp.float32)
    dqt = jnp.dot(kt, ds, preferred_element_type=jnp.float32)
    return dk, dv, dqt


NS = 16
COUNTS = (1, 1, 2, 2, 2)


def kernel(info, a0, a1, a2, a3, a4, q0, q1, q2, q3, d_own, d_mate,
           st0, st1, st2, st3, g0, g1, g2, g3, g4, dq_own, dq_mate, qs, dos, kk, vv, kt, dka, dva, dqt, lse, delta):
    x_hi = info[8]
    for rel, st in enumerate((st0, st1, st2, st3)):
        lse[2 * rel:2 * rel + 2] = st[0]
        delta[2 * rel:2 * rel + 2] = st[1]
    for rel, q_src in enumerate((q0, q1, q2, q3)):
        d_src = d_own if rel < 2 else d_mate
        x_abs = x_hi if rel % 2 == 0 else 1 - x_hi
        for s in range(2):
            for h in range(G):
                dst = pl.ds((rel * 2 + s) * W + h * SP, SP)
                qs[dst, :] = q_src[s * SP:(s + 1) * SP, h * HD:(h + 1) * HD]
                dos[dst, :] = d_src[x_abs, s * SP:(s + 1) * SP, h * HD:(h + 1) * HD]

    def spans(refs):
        i = 0
        for ref, n in zip(refs, COUNTS):
            for b in range(n):
                for s in range(2):
                    place = pl.ds(pl.multiple_of(info[9 + NS + i] * SP, SP), SP)
                    yield place, ref, b, slice(s * SP, (s + 1) * SP)
                    i += 1

    for place, ref, b, rows in spans((a0, a1, a2, a3, a4)):
        kk[place, :] = ref[b, rows, :HD]
        vv[place, :] = ref[b, rows, HD:]
    for j in range(NS // 4):
        cols = slice(j * 4 * SP, (j + 1) * 4 * SP)
        kt[:, cols] = kk[cols].astype(jnp.float32).T.astype(jnp.bfloat16)
    dka[...] = jnp.zeros_like(dka)
    dva[...] = jnp.zeros_like(dva)

    def row_span(s, carry):
        span = info[s]
        count = info[9 + 2 * NS + s]
        row = pl.multiple_of(s * W, W)
        dqt[s] = jnp.zeros((HD, W), jnp.float32)

        def work(start, n, masked):
            k0, k1 = start * SP, (start + n) * SP
            kpos = qpos = None
            if masked:
                ki = lax.broadcasted_iota(jnp.int32, (n * SP, 1), 0)
                kpos = ki + info[9 + start] * SP
                for j in range(1, n):
                    kpos = jnp.where(ki >= j * SP, ki + (info[9 + start + j] - j) * SP, kpos)
                qpos = lax.broadcasted_iota(jnp.int32, (1, W), 1) % SP + span * SP
            dk, dv, dq = unit(kk[k0:k1], vv[k0:k1], kt[:, k0:k1], qs[pl.ds(row, W), :], dos[pl.ds(row, W), :],
                              lse[s], delta[s], kpos, qpos)
            dka[k0:k1] += dk
            dva[k0:k1] += dv
            dqt[s] += dq

        for c in range(NS // 8):
            whole = info[9 + 8 * c + 7] < span

            @pl.when(whole)
            def _():
                work(8 * c, 8, False)

            @pl.when(jnp.logical_not(whole))
            def _():
                for start in (8 * c, 8 * c + 4):
                    full = info[9 + start + 3] < span

                    @pl.when(full)
                    def _():
                        work(start, 4, False)

                    @pl.when((count >= start + 3) & jnp.logical_not(full))
                    def _():
                        work(start, 4, True)

                    @pl.when((count >= start + 1) & (count < start + 3))
                    def _():
                        work(start, 2, True)

        return carry

    lax.fori_loop(0, 8, row_span, 0)
    for place, ref, b, rows in spans((g0, g1, g2, g3, g4)):
        ref[b, rows, :HD] = (dka[place, :] * SC).astype(ref.dtype)
        ref[b, rows, HD:] = dva[place, :].astype(ref.dtype)
    for rel in range(4):
        x_abs = x_hi if rel % 2 == 0 else 1 - x_hi
        for s in range(2):
            t = dqt[rel * 2 + s].T * SC
            for h in range(G):
                o = t[h * SP:(h + 1) * SP, :]
                if rel < 2:
                    dq_own[x_abs, s * SP:(s + 1) * SP, h * HD:(h + 1) * HD] = o
                else:
                    dq_mate[x_abs, s * SP:(s + 1) * SP, h * HD:(h + 1) * HD] = o.astype(jnp.bfloat16)


def attend(info, keys, qs, d_own, d_mate, stats):
    vm = pl.BlockSpec(memory_space=pltpu.VMEM)
    f32 = jnp.float32
    bf16 = jnp.bfloat16
    out_shape = [jax.ShapeDtypeStruct((n, ROWS, 2 * HD), bf16 if i == 4 else f32) for i, n in enumerate(COUNTS)]
    out_shape += [jax.ShapeDtypeStruct((2, ROWS, G * HD), f32), jax.ShapeDtypeStruct((2, ROWS, G * HD), bf16)]
    scratch = [
        pltpu.VMEM((8 * W, HD), bf16),
        pltpu.VMEM((8 * W, HD), bf16),
        pltpu.VMEM((NS * SP, HD), bf16),
        pltpu.VMEM((NS * SP, HD), bf16),
        pltpu.VMEM((HD, NS * SP), bf16),
        pltpu.VMEM((NS * SP, HD), f32),
        pltpu.VMEM((NS * SP, HD), f32),
        pltpu.VMEM((8, HD, W), f32),
        pltpu.VMEM((8, 1, W), f32),
        pltpu.VMEM((8, 1, W), f32),
    ]
    return pl.pallas_call(
        kernel,
        out_shape=out_shape,
        in_specs=[pl.BlockSpec(memory_space=pltpu.SMEM)] + [vm] * 15,
        out_specs=[vm] * len(out_shape),
        scratch_shapes=scratch,
        compiler_params=pltpu.CompilerParams(vmem_limit_bytes=32 * 2**20),
        cost_estimate=pl.CostEstimate(flops=16 * 10**9, bytes_accessed=10**7, transcendentals=5 * 10**6),
    )(info, *keys, *qs, d_own, d_mate, *stats)


def prepare(grad, keys, values, out, a0):
    for x in range(2):
        for h in range(G):
            out[x * G + h] = grad[:, h * 1024:(h + 1) * 1024]
    a0[0, :, :HD] = keys[...]
    a0[0, :, HD:] = values[...]


def finish(parts, out):
    for h in range(G):
        total = parts[h].astype(jnp.float32) + parts[G + h].astype(jnp.float32)
        out[:, h * 1024:(h + 1) * 1024] = total.astype(jnp.bfloat16)


def row_stats(x_hi, grad, attn, lse, out, prod):
    bf16 = jnp.bfloat16
    for s in range(2):
        rows = slice(s * SP, (s + 1) * SP)
        for h in range(G):
            cols = slice(h * HD, (h + 1) * HD)
            prod[h * SP:(h + 1) * SP] = grad[x_hi[0], rows, cols].astype(jnp.float32) * attn[rows, cols].astype(jnp.float32)
        full = prod[...]
        high = full.astype(bf16)
        low = (full - high.astype(jnp.float32)).astype(bf16)
        ones = jnp.ones((8, HD), bf16)
        sums = lax.dot_general(ones, high, NT, preferred_element_type=jnp.float32)
        sums += lax.dot_general(ones, low, NT, preferred_element_type=jnp.float32)
        out[1, s] = sums[:1]
        out[0, s] = lse[s]


SWAP = [(0, 1), (1, 0)]
EVEN = [(z, z ^ 1) for z in range(8)]
ODD = [(z, (z + 1) % 8 if z % 2 else (z - 1) % 8) for z in range(8)]


def arrival():
    f, g = dict(EVEN), dict(ODD)
    a0 = [[z] for z in range(8)]
    a1 = [a0[f[z]] for z in range(8)]
    a2 = [a0[g[z]] + a1[g[z]] for z in range(8)]
    a3 = [a2[f[z]] for z in range(8)]
    a4 = [a3[g[z]] for z in range(8)]
    return np.array([a0[z] + a1[z] + a2[z] + a3[z] + a4[z] for z in range(8)], np.int32)


ORDER = arrival()


def mate(x):
    return lax.ppermute(x, "core", SWAP)


def across(x):
    return lax.ppermute(x, "x", SWAP)


def along(x, route):
    return lax.ppermute(x, "z", route)


def exchange(x, axes):
    return lax.all_to_all(x, axes, split_axis=0, concat_axis=0, tiled=True)


def table(span_order, row_slots, key_slots, x_hi):
    rows, keys = span_order[row_slots], span_order[key_slots]
    rank = jnp.sum(keys[None, :] < keys[:, None], axis=1)
    hot = rank[None, :] == jnp.arange(NS)[:, None]
    ordered = jnp.sum(jnp.where(hot, keys[None, :], 0), axis=1)
    count = jnp.sum(keys[None, :] <= rows[:, None], axis=1)
    return jnp.concatenate([rows, x_hi[None], ordered, rank, count]).astype(jnp.int32)


def per_device(query_rows, key_rows, value_rows, attn_output, log_norms, grad_output, span_order):
    z, x_hi, core = lax.axis_index("z"), lax.axis_index("x"), lax.axis_index("core")
    f32 = jnp.float32
    bf16 = jnp.bfloat16
    base = lambda zz, xx, cc: ((zz * 2 + xx) * 2 + cc) * 2
    row_slots = jnp.stack([base(z, xx, cc) + s for cc in (core, 1 - core) for xx in (x_hi, 1 - x_hi) for s in (0, 1)])
    key_slots = base(jnp.asarray(ORDER)[z], x_hi, core)
    key_slots = jnp.stack([key_slots, key_slots + 1], axis=1).reshape(-1)
    info = table(span_order, row_slots, key_slots, x_hi)
    vm = pl.BlockSpec(memory_space=pltpu.VMEM)
    twice, a0 = pl.pallas_call(
        prepare,
        out_shape=(jax.ShapeDtypeStruct((16, 24, 1024), bf16), jax.ShapeDtypeStruct((1, ROWS, 2 * HD), bf16)),
        in_specs=[vm] * 3,
        out_specs=(vm, vm),
    )(grad_output, key_rows, value_rows)
    grad_rows = exchange(twice, ("x", "head")).reshape(2, ROWS, 1024)
    a1 = along(a0, EVEN)
    a2 = along(jnp.concatenate([a0, a1]), ODD)
    lse = (log_norms * LOG2E).reshape(G, 2, SP).transpose(1, 0, 2).reshape(2, 1, W)
    grad_rows, a2, info, lse = lax.optimization_barrier((grad_rows, a2, info, lse))
    a3 = along(a2, EVEN)
    q_x = across(query_rows)
    q_m = mate(query_rows)
    q_mx = mate(q_x)
    stats = pl.pallas_call(
        row_stats,
        out_shape=jax.ShapeDtypeStruct((2, 2, 1, W), f32),
        in_specs=[pl.BlockSpec(memory_space=pltpu.SMEM), vm, vm, vm],
        out_specs=vm,
        scratch_shapes=[pltpu.VMEM((W, HD), f32)],
        compiler_params=pltpu.CompilerParams(vmem_limit_bytes=8 * 2**20),
    )(x_hi[None].astype(jnp.int32), grad_rows, attn_output, lse)
    stats_x = across(stats)
    stats_x, a3 = lax.optimization_barrier((stats_x, a3))
    a4 = along(a3, ODD)
    grad_mate = mate(grad_rows)
    stats = (stats, stats_x, mate(stats), mate(stats_x))
    g0, g1, g2, g3, g4, dq_own, dq_mate = attend(
        info, (a0, a1, a2, a3, a4), (query_rows, q_x, q_m, q_mx), grad_rows, grad_mate, stats)
    r = along(g4, ODD)
    dq = (dq_own + mate(dq_mate)).astype(bf16).reshape(16, 24, 1024)
    r, dq = lax.optimization_barrier((r, dq))
    dq = exchange(dq, ("x", "head"))
    t3 = (g3 + r).astype(bf16)
    t2 = (g2 + along(t3, EVEN)).astype(bf16)
    r = along(t2, ODD)
    t1 = (g1 + r[1:]).astype(bf16)
    t1, dq = lax.optimization_barrier((t1, dq))
    fin = (g0 + r[:1] + along(t1, EVEN)).astype(bf16)[0]
    grad_query = pl.pallas_call(
        finish,
        out_shape=jax.ShapeDtypeStruct((24, G * 1024), bf16),
        in_specs=[vm],
        out_specs=vm,
        compiler_params=pltpu.CompilerParams(vmem_limit_bytes=8 * 2**20),
    )(dq)
    return (grad_query, fin[:, :HD], fin[:, HD:])


def solution(mesh):
    fine = Mesh(mesh.devices.reshape(8, 2, 2, 8), ("z", "x", "core", "head"))
    ctx = ("z", "x", "core")
    return jax.shard_map(
        per_device,
        mesh=fine,
        in_specs=(
            P(ctx, "head"),
            P(ctx, "head"),
            P(ctx, "head"),
            P(ctx, "head"),
            P("head", ctx),
            P(ctx + ("head",), None),
            P(),
        ),
        out_specs=(P(ctx + ("head",), None), P(ctx, "head"), P(ctx, "head")),
        check_vma=False,
    )
```
